512 devices in a mesh: grid: 64 (over z, y_hi, core), orb: 8 (over y_lo, x).
Axes of the slice: x: 4, y: 4 (y_hi: 2, y_lo: 2; y = y_hi * 2 + y_lo), z: 16, core: 2. Of those that a mesh axis runs over, the one named last changes fastest.
Arguments:
- orbitals: bfloat16 [16384, 8192], P('grid', 'orb'), may hold values from -6 to 6
- points: int32 [4096], P('grid'), may hold values from 0 to 16383, as said below
Outputs:
- fitted: float32 [16384, 4096], P('grid', 'orb')
- gram: float32 [4096, 4096], P('grid', 'orb')
- density: float32 [4096], P('grid')
The draws below stay inside these ranges and needn't reach their ends.
Inputs may be any that keep to these rules, and one draw needn't show every extreme that they name: `points`: entries 64 * g to 64 * g + 63 are distinct grid rows of slab g, the rows 256 * g to 256 * g + 255.
All inputs are finite; a program needn't handle non-finite values.
Results may differ from the reference program's by a relative error of at most 0.0003.
Values may be sent and summed in bfloat16 or wider, within the bound.
No kernel may reach another device: no remote copies, remote signals or barrier semaphores. Data moves between devices by JAX's collectives and lax.ppermute only.
A program may use at most 64 MiB of HBM per device.

```python
import jax
import jax.numpy as jnp
from jax import lax

NORB = 8192
ROWS_DEV = 256
MU_DEV = 64
NGRID = 16384
MU = 4096
N_GRID = 64


def draw_points(key, part):
    slabs = MU // MU_DEV
    keys = jax.random.split(jax.random.fold_in(key, 17), slabs)

    def one_slab(slab_key):
        return jax.random.permutation(slab_key, ROWS_DEV)[:MU_DEV].astype(jnp.int32)
    picks = jax.vmap(one_slab)(keys)
    slab_ids = jnp.arange(slabs, dtype=jnp.int32)
    firsts = picks[:, 0]
    shifts = jnp.where(slab_ids == 0, -firsts, jnp.zeros_like(firsts))
    shifts = jnp.where(slab_ids == slabs - 1, ROWS_DEV - 1 - firsts, shifts)
    picks = jnp.mod(picks + shifts[:, None], ROWS_DEV).astype(jnp.int32)
    offsets = (slab_ids * ROWS_DEV)[:, None]
    return (picks + offsets).reshape(MU).astype(jnp.int32)


def shard_levels(key, dims, pieces, smallest, high):
    loudness, own = 1.0, jax.random.fold_in(key, 6)
    for dim, parts in pieces:
        draws = jnp.exp(jax.random.uniform(jax.random.fold_in(own, dim), (parts,), jnp.float32, smallest / len(pieces), high / len(pieces)))
        loudness = loudness * jnp.repeat(draws, dims[dim] // parts).reshape([-1 if axis == dim else 1 for axis in range(len(dims))])
    return loudness


def scatter_about(rng, dims, deviation, bound, shards=(), kind=jnp.bfloat16):
    drawn = jax.random.normal(rng, dims, jnp.float32) * deviation
    if len(shards) > 0:
        drawn = shard_levels(rng, dims, shards, -0.22, 0.18) * drawn
    return jnp.clip(drawn, min=-bound, max=bound).astype(kind)


def setup_inputs(seed: int = 0) -> dict:
    key_list = jax.random.split(jax.random.key(seed), 3)
    orbitals = scatter_about(key_list[0], (NGRID, NORB), 1.0, 6.0, ((0, 64), (1, 8)))
    points = draw_points(jax.random.fold_in(key_list[2], 71), 0)
    return {"orbitals": orbitals, "points": points}


def reference(orbitals, points):
    chosen = jnp.take(orbitals, points, axis=0)
    chosen_wide = chosen.astype(jnp.float32)
    slabs = orbitals.reshape(N_GRID, ROWS_DEV, NORB)

    def slab_pair(block):
        return jnp.dot(block.astype(jnp.float32), chosen_wide.T, precision=lax.Precision.HIGHEST)
    pair = lax.map(slab_pair, slabs).reshape(N_GRID * ROWS_DEV, MU)
    correlation = jnp.dot(chosen_wide, chosen_wide.T, precision=lax.Precision.HIGHEST)
    scale = 1.0 / jnp.sqrt(jnp.float32(NORB))
    fitted = jnp.square(pair * scale)
    diagonal_mask = jnp.arange(MU)[:, None] == jnp.arange(MU)[None, :]
    gram = jnp.where(diagonal_mask, jnp.float32(0.0), jnp.square(correlation * scale))
    density = lax.optimization_barrier(jnp.sum(chosen_wide * chosen_wide, axis=1)) / jnp.float32(NORB)
    return (fitted, gram, density)
```

```python
import jax
import jax.numpy as jnp
from jax import lax
from jax.experimental import pallas as pl
from jax.experimental.pallas import tpu as pltpu
from jax.sharding import Mesh
from jax.sharding import PartitionSpec as P

NORB = 8192
SIZES = {"zh": 4, "zl": 4, "yh": 2, "c": 2, "yl": 2, "x": 4}
AXES = tuple(SIZES)
GRID = ("zh", "zl", "yh", "c")
ORB = ("yl", "x")
PLANE = ("yh", "c", "yl", "x")
BLOCK = 168


def routes(move):
    pairs = []
    for source in range(512):
        place, rest = {}, source
        for axis in reversed(AXES):
            place[axis] = rest % SIZES[axis]
            rest //= SIZES[axis]
        move(place)
        target = 0
        for axis in AXES:
            target = target * SIZES[axis] + place[axis]
        pairs.append((source, target))
    return pairs


def along_z(step):
    def move(place):
        z = (place["zh"] * 4 + place["zl"] + step) % 16
        place["zh"], place["zl"] = z // 4, z % 4

    return routes(move)


def flip_y(bits):
    def move(place):
        y = (place["yh"] * 2 + place["yl"]) ^ bits
        place["yh"], place["yl"] = y // 2, y % 2

    return routes(move)


def flip_core(place):
    place["c"] ^= 1


def sent(value, pairs):
    return lax.ppermute(value, AXES, pairs)


def contract(left, right):
    return lax.dot_general(
        left, right, (((1,), (1,)), ((), ())), preferred_element_type=jnp.float32
    )


def products_kernel(where, own, other, here, up, across, down, dens, out):
    zl, yh, c, yl = where[0], where[1], where[2], where[3]
    for dc, rows in enumerate((own, other)):
        for dy in range(2):
            slab = jnp.bitwise_xor(yh, dy) * 2 + jnp.bitwise_xor(c, dc)
            near = rows[(0, 3)[dy]]
            far = rows[(1, 2)[dy]]
            for dz, sets in enumerate((here, up, across, down)):
                plane = lax.rem(zl + dz, 4)
                half, parity = plane // 2, lax.rem(plane, 2)
                first = sets[:, yl].reshape(128, 1024)
                second = sets[:, 1 - yl].reshape(128, 1024)
                both = contract(first, near) + contract(second, far)
                base = pl.multiple_of(parity * 80, 8)
                for zh in range(4):
                    part = both[32 * zh : 32 * zh + 32]
                    orb = zh * 2 + half
                    out[slab, orb, pl.ds(base, 32), :] = part[:, :128]
                    out[slab, orb, pl.ds(base + 32, 32), :] = part[:, 128:256]
                    cross = jnp.concatenate([part[:16, 256:320], part[16:, 256:320]], axis=1)
                    out[slab, orb, pl.ds(base + 64, 16), :] = cross
    for slab in range(4):
        for orb in range(8):
            out[slab, orb, 160:168, :] = dens[...]


def outputs_kernel(where, parts, fitted, gram, density):
    scale = 1.0 / jnp.sqrt(jnp.float32(NORB))
    yh, c, gap = where[1], where[2], where[4]
    sums = []
    for y in range(2):
        for core in range(2):
            for k in range(2):
                sums.append(
                    (parts[y, core, k, 0, :160] + parts[y, core, k, 1, :160])
                    + (parts[y, core, k, 2, :160] + parts[y, core, k, 3, :160])
                )
    for lane in range(2):
        tall = jnp.concatenate(
            [s[80 * p + 32 * lane : 80 * p + 32 * lane + 32] for p in range(2) for s in sums], axis=0
        )
        fitted[128 * lane : 128 * lane + 128, :] = jnp.square(tall.T * scale)
    pieces = []
    for p in range(2):
        for s in sums:
            block = s[80 * p + 64 : 80 * p + 80]
            pieces += [block[:, :64], block[:, 64:]]
    cross = jnp.concatenate(pieces, axis=0).T
    shape = cross.shape
    on_diagonal = (
        lax.broadcasted_iota(jnp.int32, shape, 1) - lax.broadcasted_iota(jnp.int32, shape, 0) == gap
    )
    gram[...] = jnp.where(on_diagonal, jnp.float32(0.0), jnp.square(cross * scale))
    total = jnp.zeros((8, 128), jnp.float32)
    for k in range(2):
        for j in range(4):
            total = total + parts[yh, c, k, j, 160:168]
    density[...] = total / jnp.float32(NORB)


def on_device(orbitals, points):
    rows, width = orbitals.shape
    mu_dev = points.shape[0]
    slab = lax.axis_index(GRID)
    chosen = jnp.take(orbitals, points - slab * rows, axis=0, mode="clip")
    chosen_wide = chosen.astype(jnp.float32)
    dens = jnp.sum(chosen_wide * chosen_wide, axis=1)
    dens = jnp.broadcast_to(jnp.concatenate([dens, jnp.zeros_like(dens)])[None], (8, 128))

    halves = jnp.broadcast_to(chosen.reshape(1, 2, 32, width), (4, 2, 32, width))
    mine = jnp.concatenate([orbitals, chosen], axis=0)
    from_1 = sent(mine, flip_y(1))
    from_3 = sent(mine, flip_y(3))
    here = lax.all_to_all(
        halves.reshape(8, 32, width), ("zh", "yl"), split_axis=0, concat_axis=0, tiled=True
    ).reshape(4, 2, 32, width)
    from_1, from_3, here = lax.optimization_barrier((from_1, from_3, here))
    up = sent(here, along_z(-1))
    down = sent(here, along_z(1))
    low = sent(from_3[:160], flip_y(1))
    high = sent(from_1[160:], flip_y(3))
    across = jnp.concatenate([sent(up[:2], along_z(-1)), sent(down[2:], along_z(1))], axis=0)
    own = jnp.stack([mine, from_1, from_3, jnp.concatenate([low, high], axis=0)])
    other = sent(own, routes(flip_core))

    orb = lax.axis_index(ORB)
    where = jnp.stack(
        [lax.axis_index(a) for a in ("zl", "yh", "c", "yl")] + [slab * mu_dev - orb * 512]
    ).astype(jnp.int32)
    smem = pl.BlockSpec(memory_space=pltpu.SMEM)
    vmem = pl.BlockSpec(memory_space=pltpu.VMEM)
    blocks = pl.pallas_call(
        products_kernel,
        out_shape=jax.ShapeDtypeStruct((4, 8, BLOCK, 128), jnp.float32),
        in_specs=[smem] + [vmem] * 7,
        out_specs=vmem,
        name="products",
    )(where, own, other, here, up, across, down, dens)
    parts = lax.all_to_all(
        blocks.reshape(32, BLOCK, 128), PLANE, split_axis=0, concat_axis=0, tiled=True
    ).reshape(2, 2, 2, 4, BLOCK, 128)
    fitted, gram, density = pl.pallas_call(
        outputs_kernel,
        out_shape=(
            jax.ShapeDtypeStruct((rows, 512), jnp.float32),
            jax.ShapeDtypeStruct((mu_dev, 512), jnp.float32),
            jax.ShapeDtypeStruct((8, 128), jnp.float32),
        ),
        in_specs=[smem, vmem],
        out_specs=(vmem, vmem, vmem),
        name="outputs",
    )(where, parts)
    return fitted, gram, density[0, :mu_dev]


def solution(mesh):
    torus = Mesh(mesh.devices.reshape(tuple(SIZES.values())), AXES)
    in_specs = (P(GRID, ORB), P(GRID))
    out_specs = (P(GRID, ORB), P(GRID, ORB), P(GRID))
    return jax.shard_map(
        on_device, mesh=torus, in_specs=in_specs, out_specs=out_specs, check_vma=False
    )
```

```python
import jax
import jax.numpy as jnp
from jax import lax
from jax.experimental import pallas as pl
from jax.experimental.pallas import tpu as pltpu
from jax.sharding import Mesh
from jax.sharding import PartitionSpec as P

NORB = 8192
SIZES = {"zh": 4, "zl": 4, "yh": 2, "c": 2, "yl": 2, "xh": 2, "xl": 2}
AXES = tuple(SIZES)
GRID = ("zh", "zl", "yh", "c")
ORB = ("yl", "xh", "xl")
PLANE = ("yh", "c", "yl", "xh", "xl")

PARAMS = pltpu.CompilerParams(vmem_limit_bytes=20 << 20)


def routes(move):
    pairs = []
    for source in range(512):
        place, rest = {}, source
        for axis in reversed(AXES):
            place[axis] = rest % SIZES[axis]
            rest //= SIZES[axis]
        move(place)
        target = 0
        for axis in AXES:
            target = target * SIZES[axis] + place[axis]
        pairs.append((source, target))
    return pairs


def along_z(step):
    def move(place):
        z = (place["zh"] * 4 + place["zl"] + step) % 16
        place["zh"], place["zl"] = z // 4, z % 4

    return routes(move)


def flip_y(bits):
    def move(place):
        y = (place["yh"] * 2 + place["yl"]) ^ bits
        place["yh"], place["yl"] = y // 2, y % 2

    return routes(move)


def flip_core(place):
    place["c"] ^= 1


def flip_x(place):
    place["xl"] ^= 1


def sent(value, pairs):
    return lax.ppermute(value, AXES, pairs)


def contract(left, right):
    return lax.dot_general(
        left, right, (((1,), (1,)), ((), ())), preferred_element_type=jnp.float32
    )


def products_kernel(
    where, m0, m1, m2, n0, n1, n2, here, up, down, lower, upper, dens, out, sets, stage, sems
):
    zl, yh, c, yl, xl = where[0], where[1], where[2], where[3], where[4]
    planes = ((0, (here,)), (1, (up,)), (2, (lower, upper)), (3, (down,)))
    for dyl in range(2):
        for dxl in range(2):
            run = jnp.bitwise_xor(yl, dyl) * 2 + jnp.bitwise_xor(xl, dxl)
            at = 0
            for _, blocks in planes:
                for block in blocks:
                    size = block.shape[0] * 16
                    sets[dyl * 2 + dxl, at : at + size] = block[:, run].reshape(size, 1024)
                    at += size
    copies = []
    for dc, (base, faces, beside) in enumerate(((m0, m1, m2), (n0, n1, n2))):
        for dyh in range(2):
            slab = jnp.bitwise_xor(yh, dyh) * 2 + jnp.bitwise_xor(c, dc)
            turn = dc * 2 + dyh
            own = base if dyh == 0 else faces.at[1]
            both = contract(sets[0], own[...])
            both = both + contract(sets[1], beside[2 * dyh])
            both = both + contract(sets[2], faces[2 * dyh])
            both = both + contract(sets[3], beside[2 * dyh + 1])
            for dz in range(4):
                plane = lax.rem(zl + dz, 4)
                base_row = pl.multiple_of(lax.rem(plane, 2) * 32, 32)
                for zh in range(4):
                    part = both[64 * dz + 16 * zh : 64 * dz + 16 * zh + 16]
                    orb = zh * 2 + plane // 2
                    stage[turn, orb, pl.ds(base_row, 16), :] = part[:, :128]
                    stage[turn, orb, pl.ds(base_row + 16, 16), :] = part[:, 128:]
            for orb in range(8):
                stage[turn, orb, 64:72, :] = dens[...]
            copies.append(pltpu.make_async_copy(stage.at[turn], out.at[slab], sems.at[turn]))
            copies[-1].start()
    for copy in copies:
        copy.wait()


def outputs_kernel(where, points, parts, fitted, gram, density):
    scale = 1.0 / jnp.sqrt(jnp.float32(NORB))
    yh, c, gap = where[1], where[2], where[5]
    sums = []
    for y in range(2):
        for core in range(2):
            for k in range(2):
                for j in range(2):
                    sums.append(parts[y, core, k, 0, j, :64] + parts[y, core, k, 1, j, :64])
    for parity in range(2):
        for lane in range(2):
            at = 32 * parity + 16 * lane
            tall = jnp.concatenate([s[at : at + 16] for s in sums], axis=0)
            fitted[128 * lane : 128 * lane + 128, 256 * parity : 256 * parity + 256] = jnp.square(
                tall.T * scale
            )
    for r in range(64):
        gram[r : r + 1, :] = fitted[pl.ds(jnp.bitwise_and(points[r], 255), 1), :]
    shape = gram.shape
    on_diagonal = (
        lax.broadcasted_iota(jnp.int32, shape, 1) - lax.broadcasted_iota(jnp.int32, shape, 0) == gap
    )
    gram[...] = jnp.where(on_diagonal, jnp.float32(0.0), gram[...])
    total = jnp.zeros((8, 128), jnp.float32)
    for k in range(2):
        for j in range(4):
            total = total + parts[yh, c, k, j // 2, j % 2, 64:72]
    density[...] = total[0, :64] / jnp.float32(NORB)


def program(orbitals, points):
    rows, width = orbitals.shape
    mu_dev = points.shape[0]
    slab = lax.axis_index(GRID)
    local = jnp.clip(points - slab * rows, 0, rows - 1)
    chosen = jnp.take(orbitals, local, axis=0, mode="clip")
    chosen_wide = chosen.astype(jnp.float32)
    dens = jnp.sum(chosen_wide * chosen_wide, axis=1)
    dens = jnp.broadcast_to(jnp.concatenate([dens, jnp.zeros_like(dens)])[None], (8, 128))

    quarters = jnp.broadcast_to(chosen.reshape(1, 4, 16, width), (4, 4, 16, width))
    here = lax.all_to_all(
        quarters.reshape(16, 16, width),
        ("zh", "yl", "xl"),
        split_axis=0,
        concat_axis=0,
        tiled=True,
    ).reshape(4, 4, 16, width)
    side = sent(orbitals, routes(flip_x))
    f1 = sent(orbitals, flip_y(1))
    f3 = sent(orbitals, flip_y(3))
    f2 = sent(orbitals, flip_y(2))
    n0 = sent(orbitals, routes(flip_core))
    g1 = sent(side, flip_y(1))
    g3 = sent(side, flip_y(3))
    g2 = sent(side, flip_y(2))
    up = sent(here, along_z(-1))
    down = sent(here, along_z(1))
    lower = sent(here[:2], along_z(-2))
    upper = sent(here[2:], along_z(2))
    m1 = jnp.stack([f1, f2, f3])
    m2 = jnp.stack([side, g1, g2, g3])
    n1 = sent(m1, routes(flip_core))
    n2 = sent(m2, routes(flip_core))

    orb = lax.axis_index(ORB)
    where = jnp.stack(
        [lax.axis_index(a) for a in ("zl", "yh", "c", "yl", "xl")] + [slab * mu_dev - orb * 512]
    ).astype(jnp.int32)
    smem = pl.BlockSpec(memory_space=pltpu.SMEM)
    vmem = pl.BlockSpec(memory_space=pltpu.VMEM)
    blocks = pl.pallas_call(
        products_kernel,
        out_shape=jax.ShapeDtypeStruct((4, 8, 72, 128), jnp.float32),
        in_specs=[smem] + [vmem] * 12,
        out_specs=pl.BlockSpec(memory_space=pltpu.HBM),
        scratch_shapes=[
            pltpu.VMEM((4, 256, 1024), jnp.bfloat16),
            pltpu.VMEM((4, 8, 72, 128), jnp.float32),
            pltpu.SemaphoreType.DMA((4,)),
        ],
        compiler_params=PARAMS,
        name="products",
    )(where, orbitals, m1, m2, n0, n1, n2, here, up, down, lower, upper, dens)
    parts = lax.all_to_all(
        blocks.reshape(32, 72, 128), PLANE, split_axis=0, concat_axis=0, tiled=True
    ).reshape(2, 2, 2, 2, 2, 72, 128)
    return pl.pallas_call(
        outputs_kernel,
        out_shape=(
            jax.ShapeDtypeStruct((rows, 512), jnp.float32),
            jax.ShapeDtypeStruct((mu_dev, 512), jnp.float32),
            jax.ShapeDtypeStruct((mu_dev,), jnp.float32),
        ),
        in_specs=[smem, smem, vmem],
        out_specs=(vmem, vmem, vmem),
        compiler_params=PARAMS,
        name="outputs",
    )(where, points, parts)


def solution(mesh):
    torus = Mesh(mesh.devices.reshape(tuple(SIZES.values())), AXES)
    in_specs = (P(GRID, ORB), P(GRID))
    out_specs = (P(GRID, ORB), P(GRID, ORB), P(GRID))
    return jax.shard_map(
        program, mesh=torus, in_specs=in_specs, out_specs=out_specs, check_vma=False
    )
```

```python
import jax
import jax.numpy as jnp
from jax import lax
from jax.experimental import pallas as pl
from jax.experimental.pallas import tpu as pltpu
from jax.sharding import Mesh
from jax.sharding import PartitionSpec as P

NORB = 8192
SIZES = {"zh": 4, "zl": 4, "yh": 2, "c": 2, "yl": 2, "xh": 2, "xl": 2}
AXES = tuple(SIZES)
GRID = ("zh", "zl", "yh", "c")
ORB = ("yl", "xh", "xl")
PLANE = ("yh", "c", "yl", "xh", "xl")

PARAMS = pltpu.CompilerParams(vmem_limit_bytes=16 << 20)


def routes(move):
    pairs = []
    for source in range(512):
        place, rest = {}, source
        for axis in reversed(AXES):
            place[axis] = rest % SIZES[axis]
            rest //= SIZES[axis]
        move(place)
        target = 0
        for axis in AXES:
            target = target * SIZES[axis] + place[axis]
        pairs.append((source, target))
    return pairs


def along_z(step):
    def move(place):
        z = (place["zh"] * 4 + place["zl"] + step) % 16
        place["zh"], place["zl"] = z // 4, z % 4

    return routes(move)


def flip_y(bits):
    def move(place):
        y = (place["yh"] * 2 + place["yl"]) ^ bits
        place["yh"], place["yl"] = y // 2, y % 2

    return routes(move)


def flip_core(place):
    place["c"] ^= 1


def flip_x(place):
    place["xl"] ^= 1


def sent(value, pairs):
    return lax.ppermute(value, AXES, pairs)


def contract(left, right):
    return lax.dot_general(
        left, right, (((1,), (1,)), ((), ())), preferred_element_type=jnp.float32
    )


def pick_kernel(points, orbitals, out):
    row = lax.broadcasted_iota(jnp.int32, (256, 64), 0)
    hot = (row == jnp.bitwise_and(points[...], 255)).astype(jnp.bfloat16)
    rows = lax.dot_general(
        hot, orbitals[...], (((0,), (0,)), ((), ())), preferred_element_type=jnp.float32
    ).astype(jnp.bfloat16)
    for zh in range(4):
        for k in range(4):
            out[zh, k] = rows[16 * k : 16 * k + 16]


def slab_products(where, turn, groups, sets, dens, stage, out, sems):
    zl, yh, c = where[0], where[1], where[2]
    copies = []
    for dyh, group in enumerate(groups):
        slab = jnp.bitwise_xor(yh, dyh) * 2 + jnp.bitwise_xor(c, turn)
        both = None
        for k, piece in enumerate(group):
            part = contract(sets[k], piece[...])
            both = part if both is None else both + part
        for dz in range(4):
            plane = lax.rem(zl + dz, 4)
            base_row = pl.multiple_of(lax.rem(plane, 2) * 32, 32)
            for zh in range(4):
                part = both[64 * dz + 16 * zh : 64 * dz + 16 * zh + 16]
                orb = zh * 2 + plane // 2
                stage[dyh, orb, pl.ds(base_row, 16), :] = part[:, :128]
                stage[dyh, orb, pl.ds(base_row + 16, 16), :] = part[:, 128:]
        for orb in range(8):
            stage[dyh, orb, 64:72, :] = dens[...]
        copies.append(pltpu.make_async_copy(stage.at[dyh], out.at[slab], sems.at[dyh]))
        copies[-1].start()
    return copies


def own_kernel(where, m0, m1, mf, mh, mg, here, up, down, lower, upper, dens, na, nf, nh, out, xs, kept, *scratch):
    sets, stage, sems = scratch
    yl, xl = where[3], where[4]
    copies = []
    for piece, at, size in ((na, 0, 2), (nf, 2, 3), (nh, 5, 2)):
        copies.append(pltpu.make_async_copy(piece, xs.at[pl.ds(at, size)], sems.at[2 + at]))
        copies[-1].start()
    planes = ((here,), (up,), (lower, upper), (down,))
    for dxl in range(2):
        for dyl in range(2):
            run = jnp.bitwise_xor(yl, dyl) * 2 + jnp.bitwise_xor(xl, dxl)
            at = 0
            for blocks in planes:
                for block in blocks:
                    size = block.shape[0] * 16
                    sets[dxl * 2 + dyl, at : at + size] = block[:, run].reshape(size, 1024)
                    at += size
    copies.append(pltpu.make_async_copy(sets, kept, sems.at[3]))
    copies[-1].start()
    groups = ((m0, mf.at[0], m1, mh.at[0]), (mf.at[1], mf.at[2], mg, mh.at[1]))
    copies += slab_products(where, 0, groups, sets, dens, stage, out, sems)
    for copy in copies:
        copy.wait()


def other_kernel(where, xs, ng, kept, dens, _, out, stage, sems):
    groups = (
        (xs.at[0], xs.at[2], xs.at[1], xs.at[5]),
        (xs.at[3], xs.at[4], ng, xs.at[6]),
    )
    for copy in slab_products(where, 1, groups, kept, dens, stage, out, sems):
        copy.wait()


def outputs_kernel(where, points, parts, fitted, gram, density):
    scale = 1.0 / jnp.sqrt(jnp.float32(NORB))
    yh, c, gap = where[1], where[2], where[5]
    sums = []
    for y in range(2):
        for core in range(2):
            for k in range(2):
                for j in range(2):
                    sums.append(parts[y, core, k, 0, j, :64] + parts[y, core, k, 1, j, :64])
    for parity in range(2):
        for lane in range(2):
            at = 32 * parity + 16 * lane
            tall = jnp.concatenate([s[at : at + 16] for s in sums], axis=0)
            fitted[128 * lane : 128 * lane + 128, 256 * parity : 256 * parity + 256] = jnp.square(
                tall.T * scale
            )
    for r in range(64):
        gram[r : r + 1, :] = fitted[pl.ds(jnp.bitwise_and(points[r], 255), 1), :]
    shape = gram.shape
    on_diagonal = (
        lax.broadcasted_iota(jnp.int32, shape, 1) - lax.broadcasted_iota(jnp.int32, shape, 0) == gap
    )
    gram[...] = jnp.where(on_diagonal, jnp.float32(0.0), gram[...])
    total = jnp.zeros((8, 128), jnp.float32)
    for k in range(2):
        for j in range(4):
            total = total + parts[yh, c, k, j // 2, j % 2, 64:72]
    density[...] = total[0, :64] / jnp.float32(NORB)


def program(orbitals, points):
    rows, width = orbitals.shape
    mu_dev = points.shape[0]
    slab = lax.axis_index(GRID)
    quarters = pl.pallas_call(
        pick_kernel,
        out_shape=jax.ShapeDtypeStruct((4, 4, 16, width), orbitals.dtype),
        compiler_params=PARAMS,
        name="pick",
    )(points.reshape(1, mu_dev), orbitals)
    chosen_wide = quarters[0].reshape(mu_dev, width).astype(jnp.float32)
    dens = jnp.sum(chosen_wide * chosen_wide, axis=1)
    dens = jnp.broadcast_to(jnp.concatenate([dens, jnp.zeros_like(dens)])[None], (8, 128))

    here = lax.all_to_all(
        quarters.reshape(16, 16, width),
        ("zh", "yl", "xl"),
        split_axis=0,
        concat_axis=0,
        tiled=True,
    ).reshape(4, 4, 16, width)
    side = sent(orbitals, routes(flip_x))
    f2 = sent(orbitals, flip_y(2))
    f1 = sent(orbitals, flip_y(1))
    f3 = sent(orbitals, flip_y(3))
    g1 = sent(side, flip_y(1))
    g3 = sent(side, flip_y(3))
    mg = sent(side, flip_y(2))
    ma = jnp.stack([orbitals, side])
    na = sent(ma, routes(flip_core))
    up = sent(here, along_z(-1))
    down = sent(here, along_z(1))
    cuts = here[:2], here[2:]
    lower = sent(cuts[0], along_z(-2))
    upper = sent(cuts[1], along_z(2))
    mf = jnp.stack([f1, f2, f3])
    nf = sent(mf, routes(flip_core))
    mh = jnp.stack([g1, g3])
    nh = sent(mh, routes(flip_core))
    ng = sent(mg, routes(flip_core))

    orb = lax.axis_index(ORB)
    where = jnp.stack(
        [lax.axis_index(a) for a in ("zl", "yh", "c", "yl", "xl")] + [slab * mu_dev - orb * 512]
    ).astype(jnp.int32)
    smem = pl.BlockSpec(memory_space=pltpu.SMEM)
    vmem = pl.BlockSpec(memory_space=pltpu.VMEM)
    anywhere = pl.BlockSpec(memory_space=pl.ANY)
    shape = jax.ShapeDtypeStruct((4, 8, 72, 128), jnp.float32)
    blocks, xs, kept = pl.pallas_call(
        own_kernel,
        out_shape=(
            shape,
            jax.ShapeDtypeStruct((7, rows, width), orbitals.dtype),
            jax.ShapeDtypeStruct((4, 256, width), orbitals.dtype),
        ),
        in_specs=[smem] + [vmem] * 11 + [anywhere] * 3,
        out_specs=(anywhere,) * 3,
        scratch_shapes=[
            pltpu.VMEM((4, 256, width), orbitals.dtype),
            pltpu.VMEM((2, 8, 72, 128), jnp.float32),
            pltpu.SemaphoreType.DMA((8,)),
        ],
        compiler_params=PARAMS,
        name="own_products",
    )(where, orbitals, side, mf, mh, mg, here, up, down, lower, upper, dens, na, nf, nh)
    blocks = pl.pallas_call(
        other_kernel,
        out_shape=shape,
        in_specs=[smem] + [vmem] * 4 + [anywhere],
        out_specs=anywhere,
        scratch_shapes=[
            pltpu.VMEM((2, 8, 72, 128), jnp.float32),
            pltpu.SemaphoreType.DMA((2,)),
        ],
        input_output_aliases={5: 0},
        compiler_params=PARAMS,
        name="other_products",
    )(where, xs, ng, kept, dens, blocks)
    parts = lax.all_to_all(
        blocks.reshape(32, 72, 128), PLANE, split_axis=0, concat_axis=0, tiled=True
    ).reshape(2, 2, 2, 2, 2, 72, 128)
    return pl.pallas_call(
        outputs_kernel,
        out_shape=(
            jax.ShapeDtypeStruct((rows, 512), jnp.float32),
            jax.ShapeDtypeStruct((mu_dev, 512), jnp.float32),
            jax.ShapeDtypeStruct((mu_dev,), jnp.float32),
        ),
        in_specs=[smem, smem, vmem],
        out_specs=(vmem, vmem, vmem),
        compiler_params=PARAMS,
        name="outputs",
    )(where, points, parts)


def solution(mesh):
    torus = Mesh(mesh.devices.reshape(tuple(SIZES.values())), AXES)
    in_specs = (P(GRID, ORB), P(GRID))
    out_specs = (P(GRID, ORB), P(GRID, ORB), P(GRID))
    return jax.shard_map(
        program, mesh=torus, in_specs=in_specs, out_specs=out_specs, check_vma=False
    )
```

```python
import jax
import jax.numpy as jnp
from jax import lax
from jax.experimental import pallas as pl
from jax.experimental.pallas import tpu as pltpu
from jax.sharding import Mesh
from jax.sharding import PartitionSpec as P

NORB = 8192
SIZES = {"zh": 4, "zl": 4, "yh": 2, "c": 2, "yl": 2, "xh": 2, "xl": 2}
AXES = tuple(SIZES)
GRID = ("zh", "zl", "yh", "c")
ORB = ("yl", "xh", "xl")
PLANE = ("yh", "c", "yl", "xh", "xl")

PARAMS = pltpu.CompilerParams(vmem_limit_bytes=16 << 20)


def routes(move):
    pairs = []
    for source in range(512):
        place, rest = {}, source
        for axis in reversed(AXES):
            place[axis] = rest % SIZES[axis]
            rest //= SIZES[axis]
        move(place)
        target = 0
        for axis in AXES:
            target = target * SIZES[axis] + place[axis]
        pairs.append((source, target))
    return pairs


def along_z(step):
    def move(place):
        z = (place["zh"] * 4 + place["zl"] + step) % 16
        place["zh"], place["zl"] = z // 4, z % 4

    return routes(move)


def along_z_by_core(step):
    def move(place):
        way = step if place["c"] else -step
        z = (place["zh"] * 4 + place["zl"] + way) % 16
        place["zh"], place["zl"] = z // 4, z % 4

    return routes(move)


def flip_y(bits):
    def move(place):
        y = (place["yh"] * 2 + place["yl"]) ^ bits
        place["yh"], place["yl"] = y // 2, y % 2

    return routes(move)


def flip_core(place):
    place["c"] ^= 1


def flip_x(place):
    place["xl"] ^= 1


def sent(value, pairs):
    return lax.ppermute(value, AXES, pairs)


def contract(left, right):
    return lax.dot_general(
        left, right, (((1,), (1,)), ((), ())), preferred_element_type=jnp.float32
    )


def pick_kernel(points, orbitals, out):
    row = lax.broadcasted_iota(jnp.int32, (256, 64), 0)
    hot = (row == jnp.bitwise_and(points[...], 255)).astype(jnp.bfloat16)
    rows = lax.dot_general(
        hot, orbitals[...], (((0,), (0,)), ((), ())), preferred_element_type=jnp.float32
    ).astype(jnp.bfloat16)
    for zh in range(4):
        for k in range(4):
            out[zh, k] = rows[16 * k : 16 * k + 16]


def slab_products(where, turn, groups, sets, dens, stage, out, sems):
    zl, yh, c = where[0], where[1], where[2]
    copies = []
    for dyh, group in enumerate(groups):
        slab = jnp.bitwise_xor(yh, dyh) * 2 + jnp.bitwise_xor(c, turn)
        both = None
        for k, piece in enumerate(group):
            part = contract(sets[k], piece[...])
            both = part if both is None else both + part
        for dz in range(4):
            plane = lax.rem(zl + dz, 4)
            base_row = pl.multiple_of(lax.rem(plane, 2) * 32, 32)
            for zh in range(4):
                part = both[64 * dz + 16 * zh : 64 * dz + 16 * zh + 16]
                orb = zh * 2 + plane // 2
                stage[dyh, orb, pl.ds(base_row, 16), :] = part[:, :128]
                stage[dyh, orb, pl.ds(base_row + 16, 16), :] = part[:, 128:]
        for orb in range(8):
            stage[dyh, orb, 64:72, :] = dens[...]
        copies.append(pltpu.make_async_copy(stage.at[dyh], out.at[slab], sems.at[dyh]))
        copies[-1].start()
    return copies


def own_kernel(where, ma, mf, mh, mg, here, up, two, down, dens, na, nf, nh, out, xs, kept, *scratch):
    sets, stage, sems = scratch
    yl, xl = where[3], where[4]
    copies = []
    for piece, target, at in ((na, xs.at[:2], 2), (nf, xs.at[2:6], 4), (nh, xs.at[6], 5)):
        copies.append(pltpu.make_async_copy(piece, target, sems.at[at]))
        copies[-1].start()
    planes = (here, up, two, down)
    for dxl in range(2):
        for dyl in range(2):
            run = jnp.bitwise_xor(yl, dyl) * 2 + jnp.bitwise_xor(xl, dxl)
            at = 0
            for block in planes:
                sets[dxl * 2 + dyl, at : at + 64] = block[:, run].reshape(64, 1024)
                at += 64
    copies.append(pltpu.make_async_copy(sets, kept, sems.at[3]))
    copies[-1].start()
    groups = ((ma.at[0], mf.at[0], ma.at[1], mf.at[3]), (mf.at[1], mf.at[2], mg, mh))
    copies += slab_products(where, 0, groups, sets, dens, stage, out, sems)
    for copy in copies:
        copy.wait()


def other_kernel(where, xs, ng, kept, dens, _, out, stage, sems):
    groups = (
        (xs.at[0], xs.at[2], xs.at[1], xs.at[5]),
        (xs.at[3], xs.at[4], ng, xs.at[6]),
    )
    for copy in slab_products(where, 1, groups, kept, dens, stage, out, sems):
        copy.wait()


def outputs_kernel(where, points, parts, fitted, gram, density):
    scale = 1.0 / jnp.sqrt(jnp.float32(NORB))
    yh, c, gap = where[1], where[2], where[5]
    sums = []
    for y in range(2):
        for core in range(2):
            for k in range(2):
                for j in range(2):
                    sums.append(parts[y, core, k, 0, j, :64] + parts[y, core, k, 1, j, :64])
    for parity in range(2):
        for lane in range(2):
            at = 32 * parity + 16 * lane
            tall = jnp.concatenate([s[at : at + 16] for s in sums], axis=0)
            fitted[128 * lane : 128 * lane + 128, 256 * parity : 256 * parity + 256] = jnp.square(
                tall.T * scale
            )
    for r in range(64):
        gram[r : r + 1, :] = fitted[pl.ds(jnp.bitwise_and(points[r], 255), 1), :]
    shape = gram.shape
    on_diagonal = (
        lax.broadcasted_iota(jnp.int32, shape, 1) - lax.broadcasted_iota(jnp.int32, shape, 0) == gap
    )
    gram[...] = jnp.where(on_diagonal, jnp.float32(0.0), gram[...])
    total = jnp.zeros((8, 128), jnp.float32)
    for k in range(2):
        for j in range(4):
            total = total + parts[yh, c, k, j // 2, j % 2, 64:72]
    density[...] = total[0, :64] / jnp.float32(NORB)


def program(orbitals, points):
    rows, width = orbitals.shape
    mu_dev = points.shape[0]
    slab = lax.axis_index(GRID)
    quarters = pl.pallas_call(
        pick_kernel,
        out_shape=jax.ShapeDtypeStruct((4, 4, 16, width), orbitals.dtype),
        compiler_params=PARAMS,
        name="pick",
    )(points.reshape(1, mu_dev), orbitals)
    chosen_wide = quarters[0].reshape(mu_dev, width).astype(jnp.float32)
    dens = jnp.sum(chosen_wide * chosen_wide, axis=1)
    dens = jnp.broadcast_to(jnp.concatenate([dens, jnp.zeros_like(dens)])[None], (8, 128))

    here = lax.all_to_all(
        quarters.reshape(16, 16, width),
        ("zh", "yl", "xl"),
        split_axis=0,
        concat_axis=0,
        tiled=True,
    ).reshape(4, 4, 16, width)
    side = sent(orbitals, routes(flip_x))
    f2 = sent(orbitals, flip_y(2))
    f1 = sent(orbitals, flip_y(1))
    f3 = sent(orbitals, flip_y(3))
    g1 = sent(side, flip_y(1))
    g3 = sent(side, flip_y(3))
    ma = jnp.stack([orbitals, side])
    na = sent(ma, routes(flip_core))
    up = sent(here, along_z(-1))
    down = sent(here, along_z(1))
    two = sent(here, along_z_by_core(2))
    mg = sent(f2, routes(flip_x))
    mf = jnp.stack([f1, f2, f3, g1])
    nf = sent(mf, routes(flip_core))
    nh = sent(g3, routes(flip_core))
    ng = sent(mg, routes(flip_core))

    orb = lax.axis_index(ORB)
    where = jnp.stack(
        [lax.axis_index(a) for a in ("zl", "yh", "c", "yl", "xl")] + [slab * mu_dev - orb * 512]
    ).astype(jnp.int32)
    smem = pl.BlockSpec(memory_space=pltpu.SMEM)
    vmem = pl.BlockSpec(memory_space=pltpu.VMEM)
    anywhere = pl.BlockSpec(memory_space=pl.ANY)
    shape = jax.ShapeDtypeStruct((4, 8, 72, 128), jnp.float32)
    blocks, xs, kept = pl.pallas_call(
        own_kernel,
        out_shape=(
            shape,
            jax.ShapeDtypeStruct((7, rows, width), orbitals.dtype),
            jax.ShapeDtypeStruct((4, 256, width), orbitals.dtype),
        ),
        in_specs=[smem] + [vmem] * 9 + [anywhere] * 3,
        out_specs=(anywhere,) * 3,
        scratch_shapes=[
            pltpu.VMEM((4, 256, width), orbitals.dtype),
            pltpu.VMEM((2, 8, 72, 128), jnp.float32),
            pltpu.SemaphoreType.DMA((8,)),
        ],
        compiler_params=PARAMS,
        name="own_products",
    )(where, ma, mf, g3, mg, here, up, two, down, dens, na, nf, nh)
    blocks = pl.pallas_call(
        other_kernel,
        out_shape=shape,
        in_specs=[smem] + [vmem] * 4 + [anywhere],
        out_specs=anywhere,
        scratch_shapes=[
            pltpu.VMEM((2, 8, 72, 128), jnp.float32),
            pltpu.SemaphoreType.DMA((2,)),
        ],
        input_output_aliases={5: 0},
        compiler_params=PARAMS,
        name="other_products",
    )(where, xs, ng, kept, dens, blocks)
    parts = lax.all_to_all(
        blocks.reshape(32, 72, 128), PLANE, split_axis=0, concat_axis=0, tiled=True
    ).reshape(2, 2, 2, 2, 2, 72, 128)
    return pl.pallas_call(
        outputs_kernel,
        out_shape=(
            jax.ShapeDtypeStruct((rows, 512), jnp.float32),
            jax.ShapeDtypeStruct((mu_dev, 512), jnp.float32),
            jax.ShapeDtypeStruct((mu_dev,), jnp.float32),
        ),
        in_specs=[smem, smem, vmem],
        out_specs=(vmem, vmem, vmem),
        compiler_params=PARAMS,
        name="outputs",
    )(where, points, parts)


def solution(mesh):
    torus = Mesh(mesh.devices.reshape(tuple(SIZES.values())), AXES)
    in_specs = (P(GRID, ORB), P(GRID))
    out_specs = (P(GRID, ORB), P(GRID, ORB), P(GRID))
    return jax.shard_map(
        program, mesh=torus, in_specs=in_specs, out_specs=out_specs, check_vma=False
    )
```

```python
import jax
import jax.numpy as jnp
from jax import lax
from jax.experimental import pallas as pl
from jax.experimental.pallas import tpu as pltpu
from jax.sharding import Mesh
from jax.sharding import PartitionSpec as P

NORB = 8192
SIZES = {"zh": 4, "zl": 4, "yh": 2, "c": 2, "yl": 2, "xh": 2, "xl": 2}
AXES = tuple(SIZES)
GRID = ("zh", "zl", "yh", "c")
ORB = ("yl", "xh", "xl")
PLANE = ("yh", "c", "yl", "xh", "xl")

PARAMS = pltpu.CompilerParams(vmem_limit_bytes=16 << 20)


def routes(move):
    pairs = []
    for source in range(512):
        place, rest = {}, source
        for axis in reversed(AXES):
            place[axis] = rest % SIZES[axis]
            rest //= SIZES[axis]
        move(place)
        target = 0
        for axis in AXES:
            target = target * SIZES[axis] + place[axis]
        pairs.append((source, target))
    return pairs


def along_z(step):
    def move(place):
        z = (place["zh"] * 4 + place["zl"] + step) % 16
        place["zh"], place["zl"] = z // 4, z % 4

    return routes(move)


def along_z_by_core(step):
    def move(place):
        way = step if place["c"] else -step
        z = (place["zh"] * 4 + place["zl"] + way) % 16
        place["zh"], place["zl"] = z // 4, z % 4

    return routes(move)


def flip_y(bits):
    def move(place):
        y = (place["yh"] * 2 + place["yl"]) ^ bits
        place["yh"], place["yl"] = y // 2, y % 2

    return routes(move)


def flip_core(place):
    place["c"] ^= 1


def flip_x(place):
    place["xl"] ^= 1


def sent(value, pairs):
    return lax.ppermute(value, AXES, pairs)


def contract(left, right):
    return lax.dot_general(
        left, right, (((1,), (1,)), ((), ())), preferred_element_type=jnp.float32
    )


def pick_kernel(points, orbitals, out):
    row = lax.broadcasted_iota(jnp.int32, (256, 64), 0)
    hot = (row == jnp.bitwise_and(points[...], 255)).astype(jnp.bfloat16)
    rows = lax.dot_general(
        hot, orbitals[...], (((0,), (0,)), ((), ())), preferred_element_type=jnp.float32
    ).astype(jnp.bfloat16)
    for zh in range(4):
        for k in range(4):
            out[zh, k] = rows[16 * k : 16 * k + 16]


def slab_products(where, turn, groups, sets, dens, stage, out, sems):
    zl, yh, c = where[0], where[1], where[2]
    copies = []
    for dyh, group in enumerate(groups):
        slab = jnp.bitwise_xor(yh, dyh) * 2 + jnp.bitwise_xor(c, turn)
        both = None
        for k, piece in enumerate(group):
            part = contract(sets[k], piece[...])
            both = part if both is None else both + part
        for dz in range(4):
            plane = lax.rem(zl + dz, 4)
            base_row = pl.multiple_of(lax.rem(plane, 2) * 32, 32)
            for zh in range(4):
                part = both[64 * dz + 16 * zh : 64 * dz + 16 * zh + 16]
                orb = zh * 2 + plane // 2
                stage[dyh, orb, pl.ds(base_row, 16), :] = part[:, :128]
                stage[dyh, orb, pl.ds(base_row + 16, 16), :] = part[:, 128:]
        for orb in range(8):
            stage[dyh, orb, 64:72, :] = dens if dyh == 0 else jnp.zeros_like(dens)
        copies.append(pltpu.make_async_copy(stage.at[dyh], out.at[slab], sems.at[dyh]))
        copies[-1].start()
    return copies


def own_kernel(where, ma, mf, mh, mg, here, up, two, down, quarters, na, nf, nh, out, xs, kept, *scratch):
    sets, stage, sems = scratch
    yl, xl = where[3], where[4]
    copies = []
    for piece, target, at in ((na, xs.at[:2], 2), (nf, xs.at[2:6], 4), (nh, xs.at[6], 5)):
        copies.append(pltpu.make_async_copy(piece, target, sems.at[at]))
        copies[-1].start()
    planes = (here, up, two, down)
    for dxl in range(2):
        for dyl in range(2):
            run = jnp.bitwise_xor(yl, dyl) * 2 + jnp.bitwise_xor(xl, dxl)
            at = 0
            for block in planes:
                sets[dxl * 2 + dyl, at : at + 64] = block[:, run].reshape(64, 1024)
                at += 64
    copies.append(pltpu.make_async_copy(sets, kept, sems.at[3]))
    copies[-1].start()
    groups = ((ma.at[0], mf.at[0], ma.at[1], mf.at[3]), (mf.at[1], mf.at[2], mg, mh))
    chosen = quarters[0].reshape(64, 1024).astype(jnp.float32)
    dens = lax.dot_general(
        jnp.ones((8, 1024), jnp.float32),
        chosen * chosen,
        (((1,), (1,)), ((), ())),
        precision=lax.Precision.HIGHEST,
        preferred_element_type=jnp.float32,
    )
    dens = jnp.concatenate([dens, jnp.zeros_like(dens)], axis=1)
    copies += slab_products(where, 0, groups, sets, dens, stage, out, sems)
    for copy in copies:
        copy.wait()


def other_kernel(where, xs, ng, kept, _, out, stage, sems):
    groups = (
        (xs.at[0], xs.at[2], xs.at[1], xs.at[5]),
        (xs.at[3], xs.at[4], ng, xs.at[6]),
    )
    for copy in slab_products(where, 1, groups, kept, jnp.zeros((8, 128), jnp.float32), stage, out, sems):
        copy.wait()


def outputs_kernel(where, points, parts, fitted, gram, density):
    scale = 1.0 / jnp.sqrt(jnp.float32(NORB))
    yh, c, gap = where[1], where[2], where[5]
    sums = []
    for y in range(2):
        for core in range(2):
            for k in range(2):
                for j in range(2):
                    sums.append(parts[y, core, k, 0, j, :64] + parts[y, core, k, 1, j, :64])
    for parity in range(2):
        for lane in range(2):
            at = 32 * parity + 16 * lane
            tall = jnp.concatenate([s[at : at + 16] for s in sums], axis=0)
            fitted[128 * lane : 128 * lane + 128, 256 * parity : 256 * parity + 256] = jnp.square(
                tall.T * scale
            )
    for r in range(64):
        gram[r : r + 1, :] = fitted[pl.ds(jnp.bitwise_and(points[r], 255), 1), :]
    shape = gram.shape
    on_diagonal = (
        lax.broadcasted_iota(jnp.int32, shape, 1) - lax.broadcasted_iota(jnp.int32, shape, 0) == gap
    )
    gram[...] = jnp.where(on_diagonal, jnp.float32(0.0), gram[...])
    total = jnp.zeros((8, 128), jnp.float32)
    for k in range(2):
        for j in range(4):
            total = total + parts[yh, c, k, j // 2, j % 2, 64:72]
    density[...] = total[0, :64] / jnp.float32(NORB)


def program(orbitals, points):
    rows, width = orbitals.shape
    mu_dev = points.shape[0]
    slab = lax.axis_index(GRID)
    quarters = pl.pallas_call(
        pick_kernel,
        out_shape=jax.ShapeDtypeStruct((4, 4, 16, width), orbitals.dtype),
        compiler_params=PARAMS,
        name="pick",
    )(points.reshape(1, mu_dev), orbitals)
    here = lax.all_to_all(
        quarters.reshape(16, 16, width),
        ("zh", "yl", "xl"),
        split_axis=0,
        concat_axis=0,
        tiled=True,
    ).reshape(4, 4, 16, width)
    side = sent(orbitals, routes(flip_x))
    f2 = sent(orbitals, flip_y(2))
    f1 = sent(orbitals, flip_y(1))
    f3 = sent(orbitals, flip_y(3))
    g1 = sent(side, flip_y(1))
    g3 = sent(side, flip_y(3))
    ma = jnp.stack([orbitals, side])
    na = sent(ma, routes(flip_core))
    up = sent(here, along_z(-1))
    down = sent(here, along_z(1))
    two = sent(here, along_z_by_core(2))
    mg = sent(f2, routes(flip_x))
    mf = jnp.stack([f1, f2, f3, g1])
    nf = sent(mf, routes(flip_core))
    nh = sent(g3, routes(flip_core))
    ng = sent(mg, routes(flip_core))

    orb = lax.axis_index(ORB)
    where = jnp.stack(
        [lax.axis_index(a) for a in ("zl", "yh", "c", "yl", "xl")] + [slab * mu_dev - orb * 512]
    ).astype(jnp.int32)
    smem = pl.BlockSpec(memory_space=pltpu.SMEM)
    vmem = pl.BlockSpec(memory_space=pltpu.VMEM)
    anywhere = pl.BlockSpec(memory_space=pl.ANY)
    shape = jax.ShapeDtypeStruct((4, 8, 72, 128), jnp.float32)
    blocks, xs, kept = pl.pallas_call(
        own_kernel,
        out_shape=(
            shape,
            jax.ShapeDtypeStruct((7, rows, width), orbitals.dtype),
            jax.ShapeDtypeStruct((4, 256, width), orbitals.dtype),
        ),
        in_specs=[smem] + [vmem] * 9 + [anywhere] * 3,
        out_specs=(anywhere,) * 3,
        scratch_shapes=[
            pltpu.VMEM((4, 256, width), orbitals.dtype),
            pltpu.VMEM((2, 8, 72, 128), jnp.float32),
            pltpu.SemaphoreType.DMA((8,)),
        ],
        compiler_params=PARAMS,
        name="own_products",
    )(where, ma, mf, g3, mg, here, up, two, down, quarters, na, nf, nh)
    blocks = pl.pallas_call(
        other_kernel,
        out_shape=shape,
        in_specs=[smem] + [vmem] * 3 + [anywhere],
        out_specs=anywhere,
        scratch_shapes=[
            pltpu.VMEM((2, 8, 72, 128), jnp.float32),
            pltpu.SemaphoreType.DMA((2,)),
        ],
        input_output_aliases={4: 0},
        compiler_params=PARAMS,
        name="other_products",
    )(where, xs, ng, kept, blocks)
    parts = lax.all_to_all(
        blocks.reshape(32, 72, 128), PLANE, split_axis=0, concat_axis=0, tiled=True
    ).reshape(2, 2, 2, 2, 2, 72, 128)
    return pl.pallas_call(
        outputs_kernel,
        out_shape=(
            jax.ShapeDtypeStruct((rows, 512), jnp.float32),
            jax.ShapeDtypeStruct((mu_dev, 512), jnp.float32),
            jax.ShapeDtypeStruct((mu_dev,), jnp.float32),
        ),
        in_specs=[smem, smem, vmem],
        out_specs=(vmem, vmem, vmem),
        compiler_params=PARAMS,
        name="outputs",
    )(where, points, parts)


def solution(mesh):
    torus = Mesh(mesh.devices.reshape(tuple(SIZES.values())), AXES)
    in_specs = (P(GRID, ORB), P(GRID))
    out_specs = (P(GRID, ORB), P(GRID, ORB), P(GRID))
    return jax.shard_map(
        program, mesh=torus, in_specs=in_specs, out_specs=out_specs, check_vma=False
    )
```
